32 devices in a mesh: dp: 16 (over z, y, x), tensor: 2 (over core).
Axes of the slice: x: 2, y: 2, z: 4, core: 2. Of those that a mesh axis runs over, the one named last changes fastest.
Arguments:
- tokens: bfloat16 [16384, 768], P(('dp', 'tensor')), may hold values from -6 to 6
- out_grad: bfloat16 [16384, 768], P(('dp', 'tensor')), may hold values from -6 to 6
- inward_weight: float32 [768, 2304], P('dp'), may hold values from -0.21875 to 0.21875
- inward_first: float32 [768, 2304], P('dp'), may hold values from -384 to 384
- inward_second: float32 [768, 2304], P('dp'), may hold values from 4096 to 16384
- outward_weight: float32 [768, 768], P('dp'), may hold values from -0.875 to 0.875
- outward_first: float32 [768, 768], P('dp'), may hold values from -96 to 96
- outward_second: float32 [768, 768], P('dp'), may hold values from 256 to 1024
- feature_weight: float32 [2, 12, 64, 64], replicated, may hold values from -2 to 2
- feature_first: float32 [2, 12, 64, 64], replicated, may hold values from -96 to 96
- feature_second: float32 [2, 12, 64, 64], replicated, may hold values from 256 to 1024
- hidden_weight: float32 [2, 768, 3072], P(None, 'dp', 'tensor'), may hold values from -0.15625 to 0.15625
- hidden_first: float32 [2, 768, 3072], P(None, 'dp', 'tensor'), may hold values from -256 to 256
- hidden_second: float32 [2, 768, 3072], P(None, 'dp', 'tensor'), may hold values from 2048 to 8192
- norm_gains: float32 [2, 768], replicated, may hold values from 0.5 to 1.5
- gains_first: float32 [2, 768], replicated, may hold values from -512 to 512
- gains_second: float32 [2, 768], replicated, may hold values from 8192 to 32768
- bias_rows: float32 [7, 768], replicated, may hold values from -3 to 3
- biases_first: float32 [7, 768], replicated, may hold values from -512 to 512
- biases_second: float32 [7, 768], replicated, may hold values from 8192 to 32768
- hidden_bias: float32 [3072], replicated, may hold values from -3 to 3
- upbias_first: float32 [3072], replicated, may hold values from -192 to 192
- upbias_second: float32 [3072], replicated, may hold values from 1024 to 4096
Outputs:
- block_out: bfloat16 [16384, 768], P(('dp', 'tensor'))
- token_grad: float32 [16384, 768], P(('dp', 'tensor'))
- new_inward: float32 [768, 2304], P('dp')
- new_inward_first: float32 [768, 2304], P('dp')
- new_inward_second: float32 [768, 2304], P('dp')
- new_outward: float32 [768, 768], P('dp')
- new_outward_first: float32 [768, 768], P('dp')
- new_outward_second: float32 [768, 768], P('dp')
- new_feature: float32 [2, 12, 64, 64], replicated
- new_feature_first: float32 [2, 12, 64, 64], replicated
- new_feature_second: float32 [2, 12, 64, 64], replicated
- new_hidden: float32 [2, 768, 3072], P(None, 'dp', 'tensor')
- new_hidden_first: float32 [2, 768, 3072], P(None, 'dp', 'tensor')
- new_hidden_second: float32 [2, 768, 3072], P(None, 'dp', 'tensor')
- new_gains: float32 [2, 768], replicated
- new_gains_first: float32 [2, 768], replicated
- new_gains_second: float32 [2, 768], replicated
- new_biases: float32 [7, 768], replicated
- new_biases_first: float32 [7, 768], replicated
- new_biases_second: float32 [7, 768], replicated
- new_upbias: float32 [3072], replicated
- new_upbias_first: float32 [3072], replicated
- new_upbias_second: float32 [3072], replicated
The draws below stay inside these ranges and needn't reach their ends.
All inputs are finite; a program needn't handle non-finite values.
Results may differ from the reference program's by a relative error of at most 0.025.
Values may be sent and summed in bfloat16 or wider, within the bound.
No kernel may reach another device: no remote copies, remote signals or barrier semaphores. Data moves between devices by JAX's collectives and lax.ppermute only.
A program may use at most 192 MiB of HBM per device.

```python
import math
import jax
import jax.numpy as jnp
from jax import lax

D = 768
H = 12
FF = 3072
HD = 64
FEAT = 128
BLOCK = 512
SEQ = 1024
TOKENS = 16384
N_DP = 16


def steps_of(rng, dims, shards, low, top_value):
    gain, own = 1.0, jax.random.fold_in(rng, 6)
    for axis_at, parts in shards:
        steps = jnp.exp(jax.random.uniform(jax.random.fold_in(own, axis_at), (parts,), jnp.float32, low / len(shards), top_value / len(shards)))
        gain = gain * jnp.repeat(steps, dims[axis_at] // parts).reshape([-1 if axis == axis_at else 1 for axis in range(len(dims))])
    return gain


def noise(key, shape, spread, reach, shards=(), kind=jnp.bfloat16):
    loudness = steps_of(key, shape, shards, -0.22, 0.18) if shards else 1.0
    values = jax.random.normal(key, shape, jnp.float32) * spread * loudness
    return jnp.minimum(jnp.maximum(values, -reach), reach).astype(kind)


def setup_inputs(seed: int = 0) -> dict:
    key_list = jax.random.split(jax.random.key(seed), 24)
    tokens = noise(key_list[0], (TOKENS, D), 1.0, 6.0, ((0, 32),))
    out_grad = noise(key_list[1], (TOKENS, D), 1.0, 6.0, ((0, 32),))
    inward_weight = noise(key_list[2], (D, 3 * D), D ** -0.5, 0.21875, ((0, 16),), jnp.float32)
    inward_first = noise(key_list[3], (D, 3 * D), ((TOKENS // 4) ** 0.5), 384.0, ((0, 16),), jnp.float32)
    inward_second = jnp.clip(jnp.exp(math.log(16384.0) - 1.3862944 * jax.random.uniform(key_list[4], (D, 3 * D), jnp.float32) ** steps_of(key_list[4], (D, 3 * D), ((0, 16),), -0.2, 0.2)), 4096.0, 16384.0)
    outward_weight = noise(key_list[5], (D, D), (max(1, D * 64 // SEQ)) ** -0.5, 0.875, ((0, 16),), jnp.float32)
    outward_first = noise(key_list[6], (D, D), (4 * N_DP ** 0.5), 96.0, ((0, 16),), jnp.float32)
    outward_second = jnp.clip(jnp.exp(math.log(1024.0) - 1.3862944 * jax.random.uniform(key_list[7], (D, D), jnp.float32) ** steps_of(key_list[7], (D, D), ((0, 16),), -0.2, 0.2)), 256.0, 1024.0)
    feature_weight = noise(key_list[8], (2, H, HD, HD), (max(1, HD // 8)) ** -0.5, 2.0, (), jnp.float32)
    feature_first = noise(key_list[9], (2, H, HD, HD), ((TOKENS // 64) ** 0.5), 96.0, (), jnp.float32)
    feature_second = jnp.clip(jnp.exp(jax.random.uniform(key_list[10], (2, H, HD, HD), jnp.float32, math.log(256.0), math.log(1024.0))), 256.0, 1024.0)
    hidden_weight = noise(key_list[11], (2, D, FF), (2 * D) ** -0.5, 0.15625, ((1, 16), (2, 2)), jnp.float32)
    hidden_first = noise(key_list[12], (2, D, FF), ((TOKENS // 8) ** 0.5), 256.0, ((1, 16), (2, 2)), jnp.float32)
    hidden_second = jnp.clip(jnp.exp(math.log(8192.0) - 1.3862944 * jax.random.uniform(key_list[13], (2, D, FF), jnp.float32) ** steps_of(key_list[13], (2, D, FF), ((1, 16), (2, 2)), -0.2, 0.2)), 2048.0, 8192.0)
    norm_gains = jnp.clip(1.0 + 0.1 * jax.random.normal(key_list[14], (2, D), jnp.float32), 0.5, 1.5)
    gains_first = noise(key_list[15], (2, D), ((TOKENS // 2) ** 0.5), 512.0, (), jnp.float32)
    gains_second = jnp.clip(jnp.exp(jax.random.uniform(key_list[16], (2, D), jnp.float32, math.log(8192.0), math.log(32768.0))), 8192.0, 32768.0)
    bias_rows = noise(key_list[17], (7, D), 0.2, 3.0, (), jnp.float32)
    biases_first = noise(key_list[18], (7, D), ((TOKENS // 2) ** 0.5), 512.0, (), jnp.float32)
    biases_second = jnp.clip(jnp.exp(jax.random.uniform(key_list[19], (7, D), jnp.float32, math.log(8192.0), math.log(32768.0))), 8192.0, 32768.0)
    hidden_bias = noise(key_list[20], (FF,), 0.2, 3.0, (), jnp.float32)
    upbias_first = noise(key_list[21], (FF,), ((TOKENS // 16) ** 0.5), 192.0, (), jnp.float32)
    upbias_second = jnp.clip(jnp.exp(jax.random.uniform(key_list[22], (FF,), jnp.float32, math.log(1024.0), math.log(4096.0))), 1024.0, 4096.0)
    return dict(tokens=tokens, out_grad=out_grad, inward_weight=inward_weight, inward_first=inward_first, inward_second=inward_second, outward_weight=outward_weight, outward_first=outward_first, outward_second=outward_second, feature_weight=feature_weight, feature_first=feature_first, feature_second=feature_second, hidden_weight=hidden_weight, hidden_first=hidden_first, hidden_second=hidden_second, norm_gains=norm_gains, gains_first=gains_first, gains_second=gains_second, bias_rows=bias_rows, biases_first=biases_first, biases_second=biases_second, hidden_bias=hidden_bias, upbias_first=upbias_first, upbias_second=upbias_second)


@jax.custom_vjp
def low(v):
    return lax.optimization_barrier(v.astype(jnp.bfloat16)).astype(jnp.float32)

@jax.custom_vjp
def low_back(v):
    return v

def low_keep(v):
    return (low(v), None)

def low_pass(kept, grad):
    return (grad,)

def back_keep(v):
    return (v, None)

def back_low(kept, grad):
    return (low(grad),)
low.defvjp(low_keep, low_pass)
low_back.defvjp(back_keep, back_low)
highest = lax.Precision.HIGHEST
norm_eps = 1e-05
beta_one = 0.5
beta_two = 0.5
adam_eps = 1e-08
step_count = 10.0
decay_rate = 0.1
rate_matrix = 0.03
rate_output = 0.1
rate_feature = 0.1
rate_vector = 0.4
rate_upbias = 0.1

def layer_norm(row_data, gain_row, shift_row):
    row_mean = lax.optimization_barrier(jnp.mean(row_data, -1, keepdims=True))
    centered = row_data - row_mean
    variance = lax.optimization_barrier(jnp.mean(centered * centered, -1, keepdims=True))
    return centered * lax.rsqrt(variance + norm_eps) * gain_row + shift_row

def feature_map(scores):
    return jnp.concatenate([jax.nn.softmax(scores, axis=-1), jax.nn.softmax(-scores, axis=-1)], axis=-1)

def gelu_tanh(values):
    return jax.nn.gelu(values, approximate=True)

def adam_step(weight, first, second, gradient, rate, decay):
    new_first = beta_one * first + (1.0 - beta_one) * gradient
    new_second = beta_two * second + (1.0 - beta_two) * gradient * gradient
    first_hat = new_first / (1.0 - beta_one ** step_count)
    second_hat = new_second / (1.0 - beta_two ** step_count)
    new_weight = weight * (1.0 - rate * decay) - rate * first_hat / (jnp.sqrt(second_hat) + adam_eps)
    return (new_weight, new_first, new_second)

def attend(feat_query, feat_key, values):
    nblocks = SEQ // BLOCK
    query_blocks = feat_query.reshape(nblocks, BLOCK, H, FEAT)
    key_blocks = feat_key.reshape(nblocks, BLOCK, H, FEAT)
    value_blocks = values.reshape(nblocks, BLOCK, H, HD)
    causal = jnp.tril(jnp.ones((BLOCK, BLOCK), jnp.bool_))

    def one_block(carry, pieces):
        memory, key_sum = carry
        query_part, key_part, value_part = pieces
        raw_scores = jnp.einsum('ihf,jhf->hij', query_part, key_part, precision=highest)
        scores = low_back(jnp.where(causal[None], raw_scores, 0.0))
        numerator = low_back(jnp.einsum('hij,jhd->ihd', low(scores), value_part, precision=highest) + jnp.einsum('ihf,hfd->ihd', query_part, low(memory), precision=highest))
        denominator = low_back(lax.optimization_barrier(jnp.sum(scores, -1)).T + lax.optimization_barrier(jnp.sum(query_part * key_sum[None], -1)))
        result = numerator / denominator[:, :, None]
        update = low_back(jnp.einsum('jhf,jhd->hfd', key_part, value_part, precision=highest))
        return ((memory + update, key_sum + lax.optimization_barrier(jnp.sum(key_part, 0))), result)
    start_state = (jnp.zeros((H, FEAT, HD), jnp.float32), jnp.zeros((H, FEAT), jnp.float32))
    _, block_outs = lax.scan(jax.checkpoint(one_block), start_state, (query_blocks, key_blocks, value_blocks))
    return block_outs.reshape(SEQ, H, HD)

def forward(params, seq_tokens):
    inward, outward, feature, hidden, gains, biases, hidden_bias = params
    normed_one = low(layer_norm(seq_tokens, gains[0], biases[0]))
    projected = low_back(jnp.dot(normed_one, low(inward), precision=highest) + jnp.concatenate([biases[2], biases[3], biases[4]]))
    queries = low(projected[:, :D]).reshape(SEQ, H, HD)
    keys = low(projected[:, D:2 * D]).reshape(SEQ, H, HD)
    values = low(projected[:, 2 * D:]).reshape(SEQ, H, HD)
    feature_low = low(feature)
    query_scores = low_back(jnp.einsum('shd,hde->she', queries, feature_low[0], precision=highest))
    key_scores = low_back(jnp.einsum('shd,hde->she', keys, feature_low[1], precision=highest))
    feat_query = low(feature_map(query_scores))
    feat_key = low(feature_map(key_scores))
    mixed = low(attend(feat_query, feat_key, values).reshape(SEQ, D))
    branch = low_back(jnp.dot(mixed, low(outward), precision=highest) + biases[5])
    resid = seq_tokens + branch
    normed_two = low(layer_norm(resid, gains[1], biases[1]))
    hidden_low = low(hidden)
    pre_act = low_back(jnp.dot(normed_two, hidden_low[0], precision=highest) + hidden_bias)
    activ = low(gelu_tanh(pre_act))
    return resid + jnp.dot(activ, hidden_low[1].T, precision=highest) + biases[6]

def reference(tokens, out_grad, inward_weight, inward_first, inward_second, outward_weight, outward_first, outward_second, feature_weight, feature_first, feature_second, hidden_weight, hidden_first, hidden_second, norm_gains, gains_first, gains_second, bias_rows, biases_first, biases_second, hidden_bias, upbias_first, upbias_second):
    params = (inward_weight, outward_weight, feature_weight, hidden_weight, norm_gains, bias_rows, hidden_bias)
    seq_inputs = tokens.astype(jnp.float32).reshape(N_DP, SEQ, D)
    seq_grads = out_grad.astype(jnp.float32).reshape(N_DP, SEQ, D)

    def per_sequence(totals, pair):
        seq_x, seq_g = pair
        result, pullback = jax.vjp(forward, params, seq_x)
        grads_weights, grads_tokens = pullback(seq_g)
        totals = jax.tree.map(jnp.add, totals, grads_weights)
        return (totals, (result.astype(jnp.bfloat16), grads_tokens))
    zero_grads = jax.tree.map(jnp.zeros_like, params)
    totals, (outputs, input_grads) = lax.scan(per_sequence, zero_grads, (seq_inputs, seq_grads))
    grad_in, grad_out, grad_feat, grad_hid, grad_gain, grad_bias, grad_up = totals
    in_w, in_m, in_v = adam_step(inward_weight, inward_first, inward_second, grad_in, rate_matrix, decay_rate)
    out_w, out_m, out_v = adam_step(outward_weight, outward_first, outward_second, grad_out, rate_output, decay_rate)
    feat_w, feat_m, feat_v = adam_step(feature_weight, feature_first, feature_second, grad_feat, rate_feature, decay_rate)
    hid_w, hid_m, hid_v = adam_step(hidden_weight, hidden_first, hidden_second, grad_hid, rate_matrix, decay_rate)
    gain_w, gain_m, gain_v = adam_step(norm_gains, gains_first, gains_second, grad_gain, rate_vector, 0.0)
    bias_w, bias_m, bias_v = adam_step(bias_rows, biases_first, biases_second, grad_bias, rate_vector, 0.0)
    up_w, up_m, up_v = adam_step(hidden_bias, upbias_first, upbias_second, grad_up, rate_upbias, 0.0)
    return (outputs.reshape(TOKENS, D), input_grads.reshape(TOKENS, D), in_w, in_m, in_v, out_w, out_m, out_v, feat_w, feat_m, feat_v, hid_w, hid_m, hid_v, gain_w, gain_m, gain_v, bias_w, bias_m, bias_v, up_w, up_m, up_v)
```

```python
import jax
import jax.numpy as jnp
from jax import lax
from jax.experimental import pallas as pl
from jax.experimental.pallas import tpu as pltpu
from jax.sharding import PartitionSpec as P

D = 768
H = 12
FF = 3072
HD = 64
FEAT = 128
BLOCK = 512


norm_eps = 1e-05
beta_one = 0.5
beta_two = 0.5
adam_eps = 1e-08
step_count = 10.0
decay_rate = 0.1
rate_matrix = 0.03
rate_output = 0.1
rate_feature = 0.1
rate_vector = 0.4
rate_upbias = 0.1


def send(value, pick):
    count, cores = (lax.axis_size("dp"), lax.axis_size("tensor"))
    routes = [
        (place * cores + core, pick(place, core) * cores + core)
        for place in range(count)
        for core in range(cores)
    ]
    return lax.ppermute(value, ("dp", "tensor"), routes)


def first_mask(core):
    return 1 + core % 2


def send_first(value):
    return send(value, lambda place, core: place ^ first_mask(core))


def send_second(value):
    return send(value, lambda place, core: place ^ (3 - first_mask(core)))


def send_far(value, step):
    return send(value, lambda place, core: place ^ (4 * step))


def from_core(value, offset):
    cores = lax.axis_size("tensor")
    return lax.ppermute(
        value, "tensor", [((core + offset) % cores, core) for core in range(cores)]
    )


def carried(parts, reverse):
    cores = lax.axis_size("tensor")
    total = jax.tree.map(jnp.zeros_like, parts)
    for step in range(1, cores):
        routes = [(core, core + step) for core in range(cores - step)]
        if reverse:
            routes = [(later, earlier) for earlier, later in routes]
        got = jax.tree.map(lambda part: lax.ppermute(part, "tensor", routes), parts)
        total = jax.tree.map(jnp.add, total, got) if step > 1 else got
    return total


def gather_steps(own):
    quarter = lax.axis_size("dp") // 4
    near = jnp.stack([own] + [send_far(own, step) for step in range(1, quarter)])
    side = send_first(near)
    rest = send_second(jnp.concatenate([near, side]))
    return (near, side, rest)


def place_blocks(groups):
    count, cores = (lax.axis_size("dp"), lax.axis_size("tensor"))
    quarter = count // 4
    rows, columns = groups[0][0].shape[1:]
    split = len(groups)

    def body(*refs):
        out, sems = refs[-2:]
        place, core = (lax.axis_index("dp"), lax.axis_index("tensor"))
        copies = []
        for offset in range(split):
            owner = lax.rem(core + offset, cores)
            first = 1 + lax.rem(owner, 2)
            masks = (0, first, 3 - first, 3)
            start = pl.multiple_of(owner * columns, 128) if split > 1 else 0
            for number, base in ((0, 0), (1, 1), (2, 2)):
                source = refs[3 * offset + number]
                for entry in range(source.shape[0]):
                    mask = masks[base + entry // quarter]
                    target = place ^ (4 * (entry % quarter)) ^ mask
                    copies.append(
                        pltpu.make_async_copy(
                            source.at[entry],
                            out.at[target, :, pl.ds(start, columns)],
                            sems.at[len(copies)],
                        )
                    )
        for copy in copies:
            copy.start()
        for copy in copies:
            copy.wait()

    flat = [piece for group in groups for piece in group]
    return pl.pallas_call(
        body,
        out_shape=jax.ShapeDtypeStruct((count, rows, columns * split), jnp.bfloat16),
        in_specs=[pl.BlockSpec(memory_space=pl.ANY)] * len(flat),
        out_specs=pl.BlockSpec(memory_space=pltpu.VMEM),
        scratch_shapes=[pltpu.SemaphoreType.DMA((count * split,))],
        cost_estimate=pl.CostEstimate(
            flops=0, transcendentals=0, bytes_accessed=4 * count * rows * columns * split
        ),
        name="place_blocks",
    )(*flat).reshape(count * rows, columns * split)


def split_of(columns):
    cores = lax.axis_size("tensor")
    return cores if columns % (128 * cores) == 0 else 1


def gather_weight(weight):
    split = split_of(weight.shape[1])
    if split == 1:
        return place_blocks([gather_steps(weight.astype(jnp.bfloat16))])
    columns = weight.shape[1] // split
    own = lax.dynamic_slice_in_dim(weight, lax.axis_index("tensor") * columns, columns, 1)
    groups = [gather_steps(own.astype(jnp.bfloat16))]
    for offset in range(1, split):
        groups.append(tuple(from_core(piece, offset) for piece in groups[0]))
    return place_blocks(groups)


def block_order():
    count = lax.axis_size("dp")
    quarter = count // 4
    place, core = (lax.axis_index("dp"), lax.axis_index("tensor"))
    first = 1 + core % 2
    spot = jnp.arange(count, dtype=jnp.int32)
    side = spot // quarter
    mask = jnp.where(side == 0, 0, jnp.where(side == 1, first, jnp.where(side == 2, 3 - first, 3)))
    return (place ^ (4 * (spot % quarter)) ^ mask).astype(jnp.int32)


def order_blocks(full, order):
    count = lax.axis_size("dp")
    half = count // 2
    rows, columns = (full.shape[0] // count, full.shape[1])
    blocks = full.reshape(count, rows, columns)

    def body(order_ref, keep_in, give_in, keep_out, give_out):
        keep_out[...] = keep_in[...]
        give_out[...] = give_in[...]

    shape = jax.ShapeDtypeStruct((half, rows, columns), full.dtype)
    return pl.pallas_call(
        body,
        out_shape=(shape, shape),
        grid_spec=pltpu.PrefetchScalarGridSpec(
            num_scalar_prefetch=1,
            grid=(half,),
            in_specs=[
                pl.BlockSpec((1, rows, columns), lambda i, order_ref: (order_ref[i], 0, 0)),
                pl.BlockSpec((1, rows, columns), lambda i, order_ref: (order_ref[i + half], 0, 0)),
            ],
            out_specs=[
                pl.BlockSpec((1, rows, columns), lambda i, order_ref: (i, 0, 0)),
                pl.BlockSpec((1, rows, columns), lambda i, order_ref: (i, 0, 0)),
            ],
        ),
        cost_estimate=pl.CostEstimate(
            flops=0, transcendentals=0, bytes_accessed=4 * full.shape[0] * columns
        ),
        name="order_blocks",
    )(order, blocks, blocks)


def low_sum(left_part, right_part):
    return (left_part.astype(jnp.float32) + right_part.astype(jnp.float32)).astype(jnp.bfloat16)


def scatter_steps(keep, give):
    quarter = lax.axis_size("dp") // 4
    half_sum = low_sum(keep, send_second(give))
    quarter_sum = low_sum(half_sum[:quarter], send_first(half_sum[quarter:]))
    total = quarter_sum[0].astype(jnp.float32)
    for step in range(1, quarter):
        total = total + send_far(quarter_sum[step], step).astype(jnp.float32)
    return total


def all_sum(value):
    quarter = lax.axis_size("dp") // 4
    kind = value.dtype

    def joined(left_part, right_part):
        return (left_part.astype(jnp.float32) + right_part.astype(jnp.float32)).astype(kind)

    value = joined(value, send_first(value))
    value = joined(value, send_second(value))
    got = [value] + [send_far(value, step) for step in range(1, quarter)]
    while len(got) > 1:
        got = [joined(got[i], got[i + 1]) for i in range(0, len(got), 2)]
    value = got[0]
    cores, step = (lax.axis_size("tensor"), 1)
    while step < cores:
        routes = [(core, core ^ step) for core in range(cores)]
        value = joined(value, lax.ppermute(value, "tensor", routes))
        step *= 2
    return value


def layer_norm(row_data, gain_row, shift_row):
    row_mean = jnp.mean(row_data, -1, keepdims=True)
    centered = row_data - row_mean
    variance = jnp.mean(centered * centered, -1, keepdims=True)
    return centered * lax.rsqrt(variance + norm_eps) * gain_row + shift_row


def feature_map(scores):
    return jnp.concatenate(
        [jax.nn.softmax(scores, axis=-1), jax.nn.softmax(-scores, axis=-1)], axis=-1
    )


def gelu_tanh(values):
    return jax.nn.gelu(values, approximate=True)


def adam_step(weight, first, second, gradient, rate, decay):
    new_first = beta_one * first + (1.0 - beta_one) * gradient
    new_second = beta_two * second + (1.0 - beta_two) * gradient * gradient
    first_hat = new_first / (1.0 - beta_one**step_count)
    second_hat = new_second / (1.0 - beta_two**step_count)
    new_weight = weight * (1.0 - rate * decay) - rate * first_hat / (
        jnp.sqrt(second_hat) + adam_eps
    )
    return (new_weight, new_first, new_second)


def contract_rows(left_part, right_part):
    return lax.dot_general(
        left_part, right_part, (((0,), (0,)), ((), ())), preferred_element_type=jnp.float32
    )


def contract_cols(left_part, right_part):
    return lax.dot_general(
        left_part, right_part, (((1,), (1,)), ((), ())), preferred_element_type=jnp.float32
    )


def shared_gradient(left_part, right_part):
    columns = right_part.shape[1]
    split = split_of(columns)
    if split == 1:
        return contract_rows(left_part, right_part)
    width = columns // split
    core = lax.axis_index("tensor")
    lefts, rights = ([left_part], [lax.dynamic_slice_in_dim(right_part, core * width, width, 1)])
    for step in range(1, split):
        lefts.append(from_core(left_part, step))
        piece = lax.dynamic_slice_in_dim(right_part, (core + step) % split * width, width, 1)
        rights.append(from_core(piece, split - step))
    return contract_rows(
        jnp.concatenate(lefts),
        jnp.concatenate([rights[0]] + [rights[split - step] for step in range(1, split)]),
    )


def spread_gradient(gradient, columns, order):
    total = scatter_steps(*order_blocks(gradient.astype(jnp.bfloat16), order))
    split = columns // gradient.shape[1]
    if split == 1:
        return total
    core = lax.axis_index("tensor")
    pieces = [total] + [from_core(total, step) for step in range(1, split)]
    ordered = []
    for target in range(split):
        pick = pieces[0]
        for step in range(1, split):
            pick = jnp.where((core + step) % split == target, pieces[step], pick)
        ordered.append(pick)
    return jnp.concatenate(ordered, 1)


def add_pair(earlier, later):
    return (earlier[0] + later[0], earlier[1] + later[1])


def mlp_rows(rows_low, hidden_use, up_use):
    pre_act = jnp.dot(rows_low, hidden_use[0], preferred_element_type=jnp.float32) + up_use
    activ = gelu_tanh(pre_act).astype(jnp.bfloat16)
    return contract_cols(activ, hidden_use[1])


def mlp_back(rows_low, grad_low, hidden_use, up_use):
    pre_act = jnp.dot(rows_low, hidden_use[0], preferred_element_type=jnp.float32) + up_use
    activ, act_pull = jax.vjp(gelu_tanh, pre_act)
    activ_low = activ.astype(jnp.bfloat16)
    grad_act = jnp.dot(grad_low, hidden_use[1], preferred_element_type=jnp.float32)
    grad_pre = act_pull(grad_act)[0].astype(jnp.bfloat16)
    grad_up = contract_rows(rows_low, grad_pre)
    grad_down = contract_rows(grad_low, activ_low)
    grad_upbias = jnp.sum(grad_pre, 0, dtype=jnp.float32)
    return (grad_pre, (grad_up, grad_down), grad_upbias)


def shards(
    tokens,
    out_grad,
    inward_weight,
    inward_first,
    inward_second,
    outward_weight,
    outward_first,
    outward_second,
    feature_weight,
    feature_first,
    feature_second,
    hidden_weight,
    hidden_first,
    hidden_second,
    norm_gains,
    gains_first,
    gains_second,
    bias_rows,
    biases_first,
    biases_second,
    hidden_bias,
    upbias_first,
    upbias_second,
):
    local_rows = tokens.shape[0]
    nblocks = local_rows // BLOCK
    columns = hidden_weight.shape[2]
    cores = lax.axis_size("tensor")
    inward_full = gather_weight(inward_weight)
    outward_full = gather_weight(outward_weight)
    hidden_rows = (
        place_blocks([gather_steps(hidden_weight[0].astype(jnp.bfloat16))]),
        place_blocks([gather_steps(hidden_weight[1].astype(jnp.bfloat16))]),
    )
    token_float = tokens.astype(jnp.float32)
    normed_one = layer_norm(token_float, norm_gains[0], bias_rows[0])
    normed_one_low = normed_one.astype(jnp.bfloat16)
    qkv_bias = jnp.concatenate([bias_rows[2], bias_rows[3], bias_rows[4]])
    projected = (
        jnp.dot(normed_one_low, inward_full, preferred_element_type=jnp.float32) + qkv_bias
    ).astype(jnp.bfloat16)
    queries = projected[:, :D].reshape(local_rows, H, HD)
    keys_low = projected[:, D : 2 * D].reshape(local_rows, H, HD)
    values_low = projected[:, 2 * D :].reshape(local_rows, H, HD)
    feature_low = feature_weight.astype(jnp.bfloat16)
    query_scores = jnp.einsum(
        "shd,hde->she", queries, feature_low[0], preferred_element_type=jnp.float32
    )
    key_scores = jnp.einsum(
        "shd,hde->she", keys_low, feature_low[1], preferred_element_type=jnp.float32
    )
    feat_query = feature_map(query_scores).astype(jnp.bfloat16)
    feat_key = feature_map(key_scores).astype(jnp.bfloat16)
    query_blocks = feat_query.reshape(nblocks, BLOCK, H, FEAT)
    key_blocks = feat_key.reshape(nblocks, BLOCK, H, FEAT)
    value_blocks = values_low.reshape(nblocks, BLOCK, H, HD)
    updates = jnp.einsum(
        "njhf,njhd->nhfd", key_blocks, value_blocks, preferred_element_type=jnp.float32
    )
    key_totals = jnp.sum(key_blocks, 1, dtype=jnp.float32)
    memory_start, keysum_start = carried((jnp.sum(updates, 0), jnp.sum(key_totals, 0)), False)
    causal = jnp.tril(jnp.ones((BLOCK, BLOCK), jnp.bool_))

    def block_forward(carry, pieces):
        memory, key_sum = carry
        query_part, key_part, value_part, update, key_total = pieces
        scores = jnp.where(
            causal[None],
            jnp.einsum("ihf,jhf->hij", query_part, key_part, preferred_element_type=jnp.float32),
            0.0,
        )
        numerator = jnp.einsum(
            "hij,jhd->ihd",
            scores.astype(jnp.bfloat16),
            value_part,
            preferred_element_type=jnp.float32,
        ) + jnp.einsum(
            "ihf,hfd->ihd",
            query_part,
            memory.astype(jnp.bfloat16),
            preferred_element_type=jnp.float32,
        )
        denominator = jnp.sum(scores, -1).T + jnp.sum(
            query_part.astype(jnp.float32) * key_sum[None], -1
        )
        return ((memory + update, key_sum + key_total), (numerator, denominator, memory, key_sum))

    _, (numerators, denominators, memories, key_sums) = lax.scan(
        block_forward,
        (memory_start, keysum_start),
        (query_blocks, key_blocks, value_blocks, updates, key_totals),
    )
    mixed = (numerators / denominators[..., None]).reshape(local_rows, D).astype(jnp.bfloat16)
    resid = (
        token_float
        + jnp.dot(mixed, outward_full, preferred_element_type=jnp.float32)
        + bias_rows[5]
    )
    normed_two_low = layer_norm(resid, norm_gains[1], bias_rows[1]).astype(jnp.bfloat16)
    col_start = lax.axis_index("tensor") * columns
    up_use = lax.dynamic_slice_in_dim(hidden_bias, col_start, columns, 0)
    all_normed = jnp.concatenate(
        [normed_two_low] + [from_core(normed_two_low, step) for step in range(1, cores)]
    )
    all_grad = jnp.concatenate([out_grad] + [from_core(out_grad, step) for step in range(1, cores)])

    def own_rows(value):
        total = value[:local_rows].astype(jnp.float32)
        for step in range(1, cores):
            piece = value[step * local_rows : (step + 1) * local_rows]
            total = total + from_core(piece, cores - step).astype(jnp.float32)
        return total

    mlp_out = own_rows(mlp_rows(all_normed, hidden_rows, up_use).astype(jnp.bfloat16))
    block_out = (resid + mlp_out + bias_rows[6]).astype(jnp.bfloat16)
    grad_pre, grad_hidden, grad_up_part = mlp_back(all_normed, all_grad, hidden_rows, up_use)
    grad_normed_two = own_rows(contract_cols(grad_pre, hidden_rows[0]))
    grad_upbias = lax.dynamic_update_slice_in_dim(
        jnp.zeros((FF,), jnp.float32), grad_up_part, col_start, 0
    )
    _, two_pull = jax.vjp(layer_norm, resid, norm_gains[1], bias_rows[1])
    grad_resid_norm, grad_gain_two, grad_shift_two = two_pull(grad_normed_two)
    grad_resid = out_grad.astype(jnp.float32) + grad_resid_norm
    grad_branch = grad_resid.astype(jnp.bfloat16)
    grad_outward = shared_gradient(mixed, grad_branch)
    grad_out_bias = jnp.sum(grad_branch, 0, dtype=jnp.float32)
    grad_mixed = contract_cols(grad_branch, outward_full).reshape(nblocks, BLOCK, H, HD)

    def block_backward(pieces):
        query_part, key_part, value_part, numerator, denominator, memory, key_sum, grad_part = (
            pieces
        )
        scores = jnp.where(
            causal[None],
            jnp.einsum("ihf,jhf->hij", query_part, key_part, preferred_element_type=jnp.float32),
            0.0,
        )
        grad_num = (grad_part / denominator[..., None]).astype(jnp.bfloat16)
        grad_den = jnp.sum(-grad_part * numerator * denominator[..., None] ** (-2), -1).astype(
            jnp.bfloat16
        )
        grad_den_float = grad_den.astype(jnp.float32)
        grad_low = jnp.einsum(
            "ihd,jhd->hij", grad_num, value_part, preferred_element_type=jnp.float32
        )
        grad_scores = jnp.where(
            causal[None],
            (grad_low + grad_den_float.T[:, :, None]).astype(jnp.bfloat16),
            jnp.zeros((), jnp.bfloat16),
        )
        grad_query = (
            jnp.einsum("hij,jhf->ihf", grad_scores, key_part, preferred_element_type=jnp.float32)
            + jnp.einsum(
                "ihd,hfd->ihf",
                grad_num,
                memory.astype(jnp.bfloat16),
                preferred_element_type=jnp.float32,
            )
            + grad_den_float[..., None] * key_sum[None]
        )
        grad_key = jnp.einsum(
            "hij,ihf->jhf", grad_scores, query_part, preferred_element_type=jnp.float32
        )
        grad_value = jnp.einsum(
            "hij,ihd->jhd",
            scores.astype(jnp.bfloat16),
            grad_num,
            preferred_element_type=jnp.float32,
        )
        grad_memory = jnp.einsum(
            "ihf,ihd->hfd", query_part, grad_num, preferred_element_type=jnp.float32
        )
        grad_keysum = jnp.sum(query_part.astype(jnp.float32) * grad_den_float[..., None], 0)
        return (grad_query, grad_key, grad_value, grad_memory, grad_keysum)

    grad_fq, grad_fk, grad_vals, grad_memories, grad_keysums = lax.map(
        block_backward,
        (
            query_blocks,
            key_blocks,
            value_blocks,
            numerators,
            denominators,
            memories,
            key_sums,
            grad_mixed,
        ),
    )
    part_memory, part_keys = (jnp.sum(grad_memories, 0), jnp.sum(grad_keysums, 0))
    later_memory, later_keys = carried(
        (part_memory.astype(jnp.bfloat16), part_keys), True
    )
    later_memory = later_memory.astype(jnp.float32)

    def block_later(carry, pieces):
        return (add_pair(carry, pieces), carry)

    _, (after_memory, after_keys) = lax.scan(
        block_later, (later_memory, later_keys), (grad_memories, grad_keysums), reverse=True
    )
    after_low = after_memory.astype(jnp.bfloat16)
    grad_fk = (
        grad_fk
        + jnp.einsum("njhd,nhfd->njhf", value_blocks, after_low, preferred_element_type=jnp.float32)
        + after_keys[:, None]
    )
    grad_vals = grad_vals + jnp.einsum(
        "njhf,nhfd->njhd", key_blocks, after_low, preferred_element_type=jnp.float32
    )
    _, query_pull = jax.vjp(feature_map, query_scores)
    _, key_pull = jax.vjp(feature_map, key_scores)
    grad_qscore = query_pull(grad_fq.reshape(local_rows, H, FEAT))[0].astype(jnp.bfloat16)
    grad_kscore = key_pull(grad_fk.reshape(local_rows, H, FEAT))[0].astype(jnp.bfloat16)
    grad_queries = jnp.einsum(
        "she,hde->shd", grad_qscore, feature_low[0], preferred_element_type=jnp.float32
    )
    grad_keys = jnp.einsum(
        "she,hde->shd", grad_kscore, feature_low[1], preferred_element_type=jnp.float32
    )
    grad_feat_query = jnp.einsum(
        "shd,she->hde", queries, grad_qscore, preferred_element_type=jnp.float32
    )
    grad_feat_key = jnp.einsum(
        "shd,she->hde", keys_low, grad_kscore, preferred_element_type=jnp.float32
    )
    grad_projected = jnp.concatenate(
        [
            grad_queries.reshape(local_rows, D),
            grad_keys.reshape(local_rows, D),
            grad_vals.reshape(local_rows, D),
        ],
        1,
    ).astype(jnp.bfloat16)
    grad_inward = shared_gradient(normed_one_low, grad_projected)
    grad_qkv_bias = jnp.sum(grad_projected, 0, dtype=jnp.float32)
    grad_normed_one = contract_cols(grad_projected, inward_full)
    _, one_pull = jax.vjp(layer_norm, token_float, norm_gains[0], bias_rows[0])
    grad_token_norm, grad_gain_one, grad_shift_one = one_pull(grad_normed_one)
    token_grad = grad_resid + grad_token_norm
    grad_gains = jnp.stack([grad_gain_one, grad_gain_two])
    grad_biases = jnp.stack(
        [
            grad_shift_one,
            grad_shift_two,
            grad_qkv_bias[:D],
            grad_qkv_bias[D : 2 * D],
            grad_qkv_bias[2 * D :],
            grad_out_bias,
            jnp.sum(out_grad, 0, dtype=jnp.float32),
        ]
    )
    grad_feature = jnp.stack([grad_feat_query, grad_feat_key])
    order = block_order()
    hidden_parts = [
        scatter_steps(*order_blocks(part.astype(jnp.bfloat16), order)) for part in grad_hidden
    ]
    grad_hidden = jnp.stack(hidden_parts)
    grad_outward = spread_gradient(grad_outward, D, order)
    grad_inward = spread_gradient(grad_inward, 3 * D, order)
    grad_feature = all_sum(grad_feature.astype(jnp.bfloat16)).astype(jnp.float32)
    packed = jnp.concatenate(
        [grad_gains.reshape(-1), grad_biases.reshape(-1), grad_upbias]
    ).reshape(-1, 128)
    packed = all_sum(packed).reshape(-1)
    grad_gains = packed[: 2 * D].reshape(2, D)
    grad_biases = packed[2 * D : 9 * D].reshape(7, D)
    grad_upbias = packed[9 * D :]
    in_w, in_m, in_v = adam_step(
        inward_weight, inward_first, inward_second, grad_inward, rate_matrix, decay_rate
    )
    out_w, out_m, out_v = adam_step(
        outward_weight, outward_first, outward_second, grad_outward, rate_output, decay_rate
    )
    feat_w, feat_m, feat_v = adam_step(
        feature_weight, feature_first, feature_second, grad_feature, rate_feature, decay_rate
    )
    hid_w, hid_m, hid_v = adam_step(
        hidden_weight, hidden_first, hidden_second, grad_hidden, rate_matrix, decay_rate
    )
    gain_w, gain_m, gain_v = adam_step(
        norm_gains, gains_first, gains_second, grad_gains, rate_vector, 0.0
    )
    bias_w, bias_m, bias_v = adam_step(
        bias_rows, biases_first, biases_second, grad_biases, rate_vector, 0.0
    )
    up_w, up_m, up_v = adam_step(
        hidden_bias, upbias_first, upbias_second, grad_upbias, rate_upbias, 0.0
    )
    return (
        block_out,
        token_grad,
        in_w,
        in_m,
        in_v,
        out_w,
        out_m,
        out_v,
        feat_w,
        feat_m,
        feat_v,
        hid_w,
        hid_m,
        hid_v,
        gain_w,
        gain_m,
        gain_v,
        bias_w,
        bias_m,
        bias_v,
        up_w,
        up_m,
        up_v,
    )


def solution(mesh):
    placed = (
        P(("dp", "tensor"), None),
        P(("dp", "tensor"), None),
        P("dp", None),
        P("dp", None),
        P("dp", None),
        P("dp", None),
        P("dp", None),
        P("dp", None),
        P(),
        P(),
        P(),
        P(None, "dp", "tensor"),
        P(None, "dp", "tensor"),
        P(None, "dp", "tensor"),
        P(),
        P(),
        P(),
        P(),
        P(),
        P(),
        P(),
        P(),
        P(),
    )
    return jax.shard_map(
        shards,
        mesh=mesh,
        in_specs=placed,
        out_specs=(
            P(("dp", "tensor"), None),
            P(("dp", "tensor"), None),
            P("dp", None),
            P("dp", None),
            P("dp", None),
            P("dp", None),
            P("dp", None),
            P("dp", None),
            P(),
            P(),
            P(),
            P(None, "dp", "tensor"),
            P(None, "dp", "tensor"),
            P(None, "dp", "tensor"),
            P(),
            P(),
            P(),
            P(),
            P(),
            P(),
            P(),
            P(),
            P(),
        ),
        check_vma=False,
    )
```

```python
import jax
import jax.numpy as jnp
from jax import lax
from jax.experimental import pallas as pl
from jax.experimental.pallas import tpu as pltpu
from jax.sharding import PartitionSpec as P


D = 768
H = 12
FF = 3072
HD = 64
FEAT = 128


norm_eps = 1e-05
beta_one = 0.5
beta_two = 0.5
adam_eps = 1e-08
step_count = 10.0
decay_rate = 0.1
rate_matrix = 0.03
rate_output = 0.1
rate_feature = 0.1
rate_vector = 0.4
rate_upbias = 0.1


def send(value, pick):
    count, cores = (lax.axis_size("dp"), lax.axis_size("tensor"))
    routes = [
        (place * cores + core, pick(place, core) * cores + core)
        for place in range(count)
        for core in range(cores)
    ]
    return lax.ppermute(value, ("dp", "tensor"), routes)


def first_mask(core):
    return 1 + core % 2


def send_first(value):
    return send(value, lambda place, core: place ^ first_mask(core))


def send_second(value):
    return send(value, lambda place, core: place ^ (3 - first_mask(core)))


def send_far(value, step):
    return send(value, lambda place, core: place ^ (4 * step))


def from_core(value, offset):
    cores = lax.axis_size("tensor")
    return lax.ppermute(
        value, "tensor", [((core + offset) % cores, core) for core in range(cores)]
    )


def carried(parts, reverse):
    cores = lax.axis_size("tensor")
    total = jax.tree.map(jnp.zeros_like, parts)
    for step in range(1, cores):
        routes = [(core, core + step) for core in range(cores - step)]
        if reverse:
            routes = [(later, earlier) for earlier, later in routes]
        got = jax.tree.map(lambda part: lax.ppermute(part, "tensor", routes), parts)
        total = jax.tree.map(jnp.add, total, got) if step > 1 else got
    return total


def split_of(columns):
    cores = lax.axis_size("tensor")
    return cores if columns % (128 * cores) == 0 else 1


def low_sum(left_part, right_part):
    return (left_part.astype(jnp.float32) + right_part.astype(jnp.float32)).astype(jnp.bfloat16)


def scatter_one(keep, give):
    return (keep, send_second(give))


def scatter_two(parts):
    quarter = lax.axis_size("dp") // 4
    half_sum = low_sum(*parts)
    return (half_sum[:quarter], send_first(half_sum[quarter:]))


def scatter_three(parts):
    quarter_sum = low_sum(*parts)
    return [quarter_sum[0]] + [
        send_far(quarter_sum[step], step) for step in range(1, quarter_sum.shape[0])
    ]


def scatter_sum(parts):
    total = parts[0].astype(jnp.float32)
    for part in parts[1:]:
        total = total + part.astype(jnp.float32)
    return total


def all_sum(mine, other):
    count, cores = (lax.axis_size("dp"), lax.axis_size("tensor"))

    def joined(left_part, right_part):
        return (left_part.astype(jnp.float32) + right_part.astype(jnp.float32)).astype(
            left_part.dtype
        )

    routes = [(place, place ^ 1) for place in range(cores)]
    mine = joined(mine, lax.ppermute(other, "tensor", routes))
    step = 1
    while 2 * step < cores:
        others = [(place, place ^ (2 * step)) for place in range(cores)]
        mine = joined(mine, lax.ppermute(mine, "tensor", others))
        step *= 2
    mine = joined(mine, send_first(mine))
    mine = joined(mine, send_second(mine))
    step = 1
    while 4 * step < count:
        mine = joined(mine, send_far(mine, step))
        step *= 2
    return (mine, lax.ppermute(mine, "tensor", routes))


def adam_step(weight, first, second, gradient, rate, decay):
    new_first = beta_one * first + (1.0 - beta_one) * gradient
    new_second = beta_two * second + (1.0 - beta_two) * gradient * gradient
    first_hat = new_first / (1.0 - beta_one**step_count)
    second_hat = new_second / (1.0 - beta_two**step_count)
    new_weight = weight * (1.0 - rate * decay) - rate * first_hat / (
        jnp.sqrt(second_hat) + adam_eps
    )
    return (new_weight, new_first, new_second)


PAD = HD + 16
room = 28 * 1024 * 1024
more_room = 40 * 1024 * 1024


def nn(left_part, right_part):
    return jnp.dot(left_part, right_part, preferred_element_type=jnp.float32)


def contract_rows(left_part, right_part):
    return lax.dot_general(
        left_part, right_part, (((0,), (0,)), ((), ())), preferred_element_type=jnp.float32
    )


def contract_cols(left_part, right_part):
    return lax.dot_general(
        left_part, right_part, (((1,), (1,)), ((), ())), preferred_element_type=jnp.float32
    )


def estimate(flops, moved, exps=0):
    return pl.CostEstimate(flops=int(flops), bytes_accessed=int(moved), transcendentals=int(exps))


def far_spec():
    return pl.BlockSpec(memory_space=pl.ANY)


def whole(count):
    return [pl.BlockSpec(memory_space=pltpu.VMEM)] * count


def place_copies(refs, out, sems, planes=False):
    count, cores = (lax.axis_size("dp"), lax.axis_size("tensor"))
    depth, width = (len(refs), refs[0].shape[0])
    split = depth * width // count
    depth = depth // split
    columns = refs[0].shape[-1]
    place, core = (lax.axis_index("dp"), lax.axis_index("tensor"))
    copies = []
    for offset in range(split):
        owner = lax.rem(core + offset, cores)
        first = 1 + lax.rem(owner, 2)
        masks = (0, first, 3 - first, 3)
        start = pl.multiple_of(owner * columns, 128) if split > 1 else 0
        for base in range(depth):
            source = refs[depth * offset + base]
            for entry in range(width):
                far, near = (base, entry) if planes else (entry, base)
                target = place ^ (4 * far) ^ masks[near]
                copies.append(
                    pltpu.make_async_copy(
                        source.at[entry],
                        out.at[target, :, pl.ds(start, columns)],
                        sems.at[len(copies)],
                    )
                )
    return copies


def placed(pieces):
    count = lax.axis_size("dp")
    rows, columns = pieces[0].shape[1:]
    split = len(pieces) * pieces[0].shape[0] // count
    return (
        pltpu.VMEM((count, rows, columns * split), jnp.bfloat16),
        pltpu.SemaphoreType.DMA((count * split,)),
    )


def start_all(copies):
    for copy in copies:
        copy.start()


def wait_all(copies):
    for copy in copies:
        copy.wait()


def flat_rows(ref, begin, width):
    part = ref[:, :, begin : begin + width]
    return part.reshape(part.shape[0] * part.shape[1], width)


def normal_parts(rows_float):
    row_mean = jnp.mean(rows_float, -1, keepdims=True)
    centered = rows_float - row_mean
    scale = lax.rsqrt(jnp.mean(centered * centered, -1, keepdims=True) + norm_eps)
    return (centered * scale, scale)


def norm_back(normal, scale, incoming, gain_row):
    scaled = incoming * gain_row
    mean_one = jnp.mean(scaled, -1, keepdims=True)
    mean_two = jnp.mean(scaled * normal, -1, keepdims=True)
    return scale * (scaled - mean_one - normal * mean_two)


def features_call(tokens, gains, biases, feature, pieces):
    rows = tokens.shape[0]
    groups = H // 4

    def body(*refs):
        tok, gain, bias, feat = refs[:4]
        sources = refs[4 : 4 + len(pieces)]
        norm_t, query_t, key_t, value_a, feat_q, feat_k, memory, blk = refs[4 + len(pieces) : -3]
        weight, sems, normed = refs[-3:]
        copies = place_copies(sources, weight, sems)
        start_all(copies)

        def norm_rows(step, carry):
            window = pl.ds(pl.multiple_of(step * 128, 128), 128)
            normal, _ = normal_parts(tok[window, :].astype(jnp.float32))
            normed[window, :] = (normal * gain[0:1, :] + bias[0:1, :]).astype(jnp.bfloat16)
            return carry

        lax.fori_loop(0, rows // 128, norm_rows, 0)
        norm_t[...] = normed[...].T
        wide = lax.broadcasted_iota(jnp.int32, (HD, 256), 1)
        tall = lax.broadcasted_iota(jnp.int32, (HD, 256), 0)
        repeat = jnp.where(wide % HD == tall, 1.0, 0.0).astype(jnp.bfloat16)
        row = lax.broadcasted_iota(jnp.int32, (256, 256), 0)
        lane = lax.broadcasted_iota(jnp.int32, (256, 256), 1)
        same = row // HD == lane // HD
        for group in range(2 * groups):
            tiled = nn(feat[group].astype(jnp.bfloat16), repeat)
            blk[group] = jnp.where(same, tiled, 0.0).astype(jnp.bfloat16)
        wait_all(copies)
        rest = jnp.where(
            lax.broadcasted_iota(jnp.int32, (16, rows), 0) == 0, 1.0, 0.0
        ).astype(jnp.bfloat16)
        for part in range(3):
            piece = nn(normed[...], flat_rows(weight, part * D, D)) + bias[2 + part : 3 + part, :]
            turned = piece.astype(jnp.bfloat16).T
            if part == 0:
                query_t[...] = turned
            elif part == 1:
                key_t[...] = turned
            else:
                value_a[:, 0:HD, :] = turned.reshape(H, HD, rows)
                for head in range(H):
                    value_a[head, HD:PAD, :] = rest
        for which, source, target in ((0, query_t, feat_q), (1, key_t, feat_k)):
            for group in range(groups):
                scores = contract_rows(
                    blk[which * groups + group], source[group * 256 : (group + 1) * 256, :]
                ).reshape(4, HD, rows)
                high = jnp.exp(scores - jnp.max(scores, 1, keepdims=True))
                less = jnp.exp(jnp.min(scores, 1, keepdims=True) - scores)
                high = high * (1.0 / jnp.sum(high, 1, keepdims=True))
                less = less * (1.0 / jnp.sum(less, 1, keepdims=True))
                target[group * 4 : group * 4 + 4, 0:HD, :] = high.astype(jnp.bfloat16)
                target[group * 4 : group * 4 + 4, HD:FEAT, :] = less.astype(jnp.bfloat16)
        for head in range(H):
            memory[head] = contract_cols(value_a[head], feat_k[head])

    low = lambda *shape: jax.ShapeDtypeStruct(shape, jnp.bfloat16)
    return pl.pallas_call(
        body,
        out_shape=(
            low(D, rows),
            low(D, rows),
            low(D, rows),
            low(H, PAD, rows),
            low(H, FEAT, rows),
            low(H, FEAT, rows),
            jax.ShapeDtypeStruct((H, PAD, FEAT), jnp.float32),
            low(2 * groups, 256, 256),
        ),
        in_specs=whole(4) + [far_spec()] * len(pieces),
        out_specs=tuple(whole(8)),
        scratch_shapes=[*placed(pieces), pltpu.VMEM((rows, D), jnp.bfloat16)],
        compiler_params=pltpu.CompilerParams(vmem_limit_bytes=room),
        cost_estimate=estimate(2 * rows * D * 3 * D, 12e6, 4 * rows * D),
        name="features",
    )(tokens, gains, biases, feature, *pieces)


def masked_scores(feat_q, feat_k_row):
    half = feat_k_row.shape[0] // 2
    early = lax.broadcasted_iota(jnp.int32, (half, half), 0)
    later = lax.broadcasted_iota(jnp.int32, (half, half), 1)
    seen = early <= later
    top = nn(feat_k_row[0:half], feat_q)
    corner = nn(feat_k_row[half:], feat_q[:, half:])
    first = jnp.where(seen, top[:, 0:half], 0.0).astype(jnp.bfloat16)
    cross = top[:, half:].astype(jnp.bfloat16)
    last = jnp.where(seen, corner, 0.0).astype(jnp.bfloat16)
    return (first, cross, last)


def attend_call(feat_q, feat_k, value_a, memory, tokens, gains, biases, pieces):
    rows = tokens.shape[0]
    half = rows // 2

    def body(*refs):
        fq, fk, va, mem, tok, gain, bias = refs[:7]
        sources = refs[7 : 7 + len(pieces)]
        mixed_t, inverse, resid, normed = refs[7 + len(pieces) : -2]
        weight, sems = refs[-2:]
        copies = place_copies(sources, weight, sems, True)
        start_all(copies)

        def one_head(head, carry):
            first, cross, last = masked_scores(fq[head], fk[head].T)
            value = va[head]
            past = nn(mem[head].astype(jnp.bfloat16), fq[head])
            left = nn(value[:, 0:half], first)
            right = nn(value[:, 0:half], cross) + nn(value[:, half:], last)
            for begin, part in ((0, left), (half, right)):
                total = part + past[:, begin : begin + half]
                down = 1.0 / total[HD : HD + 1, :]
                window = pl.ds(pl.multiple_of(head * HD, HD), HD)
                mixed_t[window, begin : begin + half] = (total[0:HD, :] * down).astype(
                    jnp.bfloat16
                )
                inverse[head, :, begin : begin + half] = down
            return carry

        lax.fori_loop(0, H, one_head, 0, unroll=2)
        wait_all(copies)
        resid[...] = contract_rows(mixed_t[...], flat_rows(weight, 0, D))

        def finish(step, carry):
            window = pl.ds(pl.multiple_of(step * 128, 128), 128)
            value = resid[window, :] + tok[window, :].astype(jnp.float32) + bias[5:6, :]
            resid[window, :] = value
            normal, _ = normal_parts(value)
            normed[window, :] = (normal * gain[1:2, :] + bias[1:2, :]).astype(jnp.bfloat16)
            return carry

        lax.fori_loop(0, rows // 128, finish, 0)

    return pl.pallas_call(
        body,
        out_shape=(
            jax.ShapeDtypeStruct((D, rows), jnp.bfloat16),
            jax.ShapeDtypeStruct((H, 1, rows), jnp.float32),
            jax.ShapeDtypeStruct((rows, D), jnp.float32),
            jax.ShapeDtypeStruct((rows, D), jnp.bfloat16),
        ),
        in_specs=whole(7) + [far_spec()] * len(pieces),
        out_specs=tuple(whole(4)),
        scratch_shapes=list(placed(pieces)),
        compiler_params=pltpu.CompilerParams(vmem_limit_bytes=room),
        cost_estimate=estimate(H * rows * rows * 400, 10e6),
        name="attend",
    )(feat_q, feat_k, value_a, memory, tokens, gains, biases, *pieces)


gelu_scale = 0.7978845608028654
gelu_cube = 0.044715


def tile_of(columns):
    for tile in (512, 384):
        if columns % tile == 0:
            return tile
    return 128


def hidden_call(normed, up_bias, pieces):
    rows = normed[0].shape[0]
    cores = len(normed)
    columns = up_bias.shape[1]
    tile = tile_of(columns)

    def body(*refs):
        norms, bias = (refs[:cores], refs[cores])
        sources = refs[cores + 1 : cores + 1 + len(pieces)]
        outs = refs[cores + 1 + len(pieces) : -2]
        up, sems = refs[-2:]
        copies = place_copies(sources, up, sems)
        start_all(copies)
        wait_all(copies)
        for step in range(cores):
            activ, slope = outs[2 * step : 2 * step + 2]
            for begin in range(0, columns, tile):
                window = slice(begin, begin + tile)
                pre = nn(norms[step][...], flat_rows(up, begin, tile)) + bias[0:1, window]
                square = pre * pre
                bent = jnp.tanh(pre * (gelu_scale + gelu_scale * gelu_cube * square))
                half_one = 0.5 + 0.5 * bent
                activ[:, window] = (pre * half_one).astype(jnp.bfloat16)
                slope[:, window] = (
                    half_one
                    + pre
                    * (half_one * (1.0 - bent))
                    * (gelu_scale + 3.0 * gelu_scale * gelu_cube * square)
                ).astype(jnp.bfloat16)

    out = jax.ShapeDtypeStruct((rows, columns), jnp.bfloat16)
    flat = pl.pallas_call(
        body,
        out_shape=(out,) * (2 * cores),
        in_specs=whole(cores + 1) + [far_spec()] * len(pieces),
        out_specs=tuple(whole(2 * cores)),
        scratch_shapes=list(placed(pieces)),
        compiler_params=pltpu.CompilerParams(vmem_limit_bytes=room),
        cost_estimate=estimate(
            2 * cores * rows * D * columns, 9e6 * cores, cores * rows * columns
        ),
        name="hidden",
    )(*normed, up_bias, *pieces)
    return [(flat[2 * step], flat[2 * step + 1]) for step in range(cores)]


def hidden_back_call(acts, grads, up_pieces, down_pieces):
    cores = len(acts)
    rows, columns = acts[0][0].shape
    tile = tile_of(columns)
    order = list(range(1, cores)) + [0]

    def body(*refs):
        sources = refs[3 * cores : 3 * cores + len(up_pieces) + len(down_pieces)]
        outs = refs[3 * cores + len(sources) : -6]
        up, up_sems, down, down_sems, out_sum, back_sum = refs[-6:]
        bias_grad = outs[-1]
        copies = place_copies(sources[: len(up_pieces)], up, up_sems)
        copies += place_copies(sources[len(up_pieces) :], down, down_sems)
        start_all(copies)
        wait_all(copies)
        for step in order:
            act, bent, grad = refs[3 * step : 3 * step + 3]
            out, back, pre_grad = outs[3 * step : 3 * step + 3]
            for begin in range(0, columns, tile):
                window = slice(begin, begin + tile)
                up_part = flat_rows(up, begin, tile)
                down_part = flat_rows(down, begin, tile)
                grad_act = nn(grad[...], down_part)
                grad_pre = (grad_act * bent[:, window].astype(jnp.float32)).astype(jnp.bfloat16)
                pre_grad[:, window] = grad_pre
                total = jnp.sum(grad_pre.astype(jnp.float32), 0, keepdims=True)
                if step == order[0]:
                    bias_grad[:, window] = total
                else:
                    bias_grad[:, window] += total
                more = contract_cols(act[:, window], down_part)
                more_back = contract_cols(grad_pre, up_part)
                if begin == 0:
                    out_sum[...] = more
                    back_sum[...] = more_back
                else:
                    out_sum[...] += more
                    back_sum[...] += more_back
            out[...] = out_sum[...].astype(out.dtype)
            back[...] = back_sum[...]

    shapes = []
    for step in range(cores):
        shapes += [
            jax.ShapeDtypeStruct((rows, D), jnp.bfloat16 if step else jnp.float32),
            jax.ShapeDtypeStruct((rows, D), jnp.float32),
            jax.ShapeDtypeStruct((rows, columns), jnp.bfloat16),
        ]
    shapes.append(jax.ShapeDtypeStruct((1, columns), jnp.float32))
    flat = pl.pallas_call(
        body,
        out_shape=tuple(shapes),
        in_specs=whole(3 * cores) + [far_spec()] * (len(up_pieces) + len(down_pieces)),
        out_specs=tuple(whole(len(shapes))),
        scratch_shapes=[
            *placed(up_pieces),
            *placed(down_pieces),
            pltpu.VMEM((rows, D), jnp.float32),
            pltpu.VMEM((rows, D), jnp.float32),
        ],
        compiler_params=pltpu.CompilerParams(vmem_limit_bytes=more_room),
        cost_estimate=estimate(6 * cores * rows * D * columns, 15e6 * cores),
        name="hidden_back",
    )(
        *[part for act, grad in zip(acts, grads) for part in (*act, grad)],
        *up_pieces,
        *down_pieces,
    )
    return [flat[3 * step : 3 * step + 3] for step in range(cores)], flat[-1]


def stack_call(parts, widths):
    rows = parts[0].shape[0]
    quarter = len(parts)

    def body(*refs):
        begin = 0
        for width, out in zip(widths, refs[quarter:]):
            for spot in range(quarter):
                out[spot] = refs[spot][:, begin : begin + width]
            begin += width

    return pl.pallas_call(
        body,
        out_shape=tuple(
            jax.ShapeDtypeStruct((quarter, rows, width), jnp.bfloat16) for width in widths
        ),
        in_specs=whole(quarter),
        out_specs=tuple(whole(len(widths))),
        compiler_params=pltpu.CompilerParams(vmem_limit_bytes=room),
        cost_estimate=estimate(0, 4 * quarter * rows * sum(widths)),
        name="stack",
    )(*parts)


def ordered_store(total, store, keep, give):
    count = lax.axis_size("dp")
    quarter = count // 4
    rows = total.shape[0] // count
    place, core = (lax.axis_index("dp"), lax.axis_index("tensor"))
    first = 1 + lax.rem(core, 2)
    store[...] = total.reshape(count, rows, total.shape[1])
    masks = (0, first, 3 - first, 3)
    for spot in range(count):
        origin = place ^ (4 * (spot % quarter)) ^ masks[spot // quarter]
        target = keep if spot < count // 2 else give
        target[spot % (count // 2)] = store[origin].astype(jnp.bfloat16)


def product_call(lefts, rights, turned):
    count = lax.axis_size("dp")
    cores = len(lefts)
    depth = lefts[0].shape[0 if turned is False else 1]
    columns = rights[0].shape[0 if turned else 1]
    tile = columns if columns in (384, 1152) else tile_of(columns)
    rows = D // count

    def body(*refs):
        left_refs, right_refs = (refs[:cores], refs[cores : 2 * cores])
        keep, give, store = refs[2 * cores : 2 * cores + 3]
        if turned:
            parts = [
                contract_cols(left[...], right[...]) for left, right in zip(left_refs, right_refs)
            ]
        elif turned is None:
            parts = [nn(left[...], right[...]) for left, right in zip(left_refs, right_refs)]
        else:
            turns = refs[2 * cores + 3 :]

            @pl.when(pl.program_id(0) == 0)
            def turn():
                for left, target in zip(left_refs, turns):
                    target[...] = left[...].T

            parts = [nn(target[...], right[...]) for target, right in zip(turns, right_refs)]
        total = parts[0]
        for part in parts[1:]:
            total = total + part
        ordered_store(total, store, keep, give)

    full = [pl.BlockSpec(left.shape, lambda i: (0, 0)) for left in lefts]
    if turned:
        moving = [pl.BlockSpec((tile, depth), lambda i: (i, 0)) for _ in rights]
    else:
        moving = [pl.BlockSpec((depth, tile), lambda i: (0, i)) for _ in rights]
    out = jax.ShapeDtypeStruct((count // 2, rows, columns), jnp.bfloat16)
    out_spec = pl.BlockSpec((count // 2, rows, tile), lambda i: (0, 0, i))
    scratch = [pltpu.VMEM((count, rows, tile), jnp.float32)]
    if turned is False:
        scratch += [pltpu.VMEM((D, depth), jnp.bfloat16)] * cores
    return pl.pallas_call(
        body,
        out_shape=(out, out),
        grid=(columns // tile,),
        in_specs=full + moving,
        out_specs=(out_spec, out_spec),
        scratch_shapes=scratch,
        compiler_params=pltpu.CompilerParams(vmem_limit_bytes=room),
        cost_estimate=estimate(
            2 * cores * depth * D * columns, 2 * (cores * depth * (D + columns) + D * columns)
        ),
    )(*lefts, *rights)


def branch_call(back_own, back_got, out_grad, resid, mixed_t, inverse, feat_q, gains, pieces):
    rows = out_grad.shape[0]

    def body(*refs):
        own, got, grad, res, mix, inv, fq, gain = refs[:8]
        sources = refs[8 : 8 + len(pieces)]
        grad_resid, branch, grad_a, memory, sums = refs[8 + len(pieces) : -3]
        weight, sems, mixed_grad = refs[-3:]
        copies = place_copies(sources, weight, sems, True)
        start_all(copies)
        sums[...] = jnp.zeros_like(sums)

        def norm_rows(step, carry):
            window = pl.ds(pl.multiple_of(step * 128, 128), 128)
            incoming = own[window, :] + got[window, :]
            plain = grad[window, :].astype(jnp.float32)
            normal, scale = normal_parts(res[window, :])
            total = plain + norm_back(normal, scale, incoming, gain[1:2, :])
            grad_resid[window, :] = total
            low = total.astype(jnp.bfloat16)
            branch[window, :] = low
            sums[0:1, :] += jnp.sum(incoming * normal, 0, keepdims=True)
            sums[1:2, :] += jnp.sum(incoming, 0, keepdims=True)
            sums[2:3, :] += jnp.sum(low.astype(jnp.float32), 0, keepdims=True)
            sums[3:4, :] += jnp.sum(plain, 0, keepdims=True)
            return carry

        lax.fori_loop(0, rows // 128, norm_rows, 0)
        wait_all(copies)
        mixed_grad[...] = contract_cols(flat_rows(weight, 0, D), branch[...])
        place = lax.broadcasted_iota(jnp.int32, (16, rows), 0)

        def one_head(head, carry):
            window = pl.ds(pl.multiple_of(head * HD, HD), HD)
            part = mixed_grad[window, :]
            down = inv[head]
            mixed = mix[window, :].astype(jnp.float32)
            grad_den = -jnp.sum(part * mixed, 0, keepdims=True) * down
            grad_a[head, 0:HD, :] = (part * down).astype(jnp.bfloat16)
            grad_a[head, HD:PAD, :] = jnp.where(place == 0, grad_den, 0.0).astype(jnp.bfloat16)
            memory[head] = contract_cols(grad_a[head], fq[head])
            return carry

        lax.fori_loop(0, H, one_head, 0, unroll=2)

    return pl.pallas_call(
        body,
        out_shape=(
            jax.ShapeDtypeStruct((rows, D), jnp.float32),
            jax.ShapeDtypeStruct((rows, D), jnp.bfloat16),
            jax.ShapeDtypeStruct((H, PAD, rows), jnp.bfloat16),
            jax.ShapeDtypeStruct((H, PAD, FEAT), jnp.float32),
            jax.ShapeDtypeStruct((8, D), jnp.float32),
        ),
        in_specs=whole(8) + [far_spec()] * len(pieces),
        out_specs=tuple(whole(5)),
        scratch_shapes=[*placed(pieces), pltpu.VMEM((D, rows), jnp.float32)],
        compiler_params=pltpu.CompilerParams(vmem_limit_bytes=room),
        cost_estimate=estimate(2 * rows * D * D * 2, 12e6),
        name="branch",
    )(back_own, back_got, out_grad, resid, mixed_t, inverse, feat_q, gains, *pieces)


def soft_back(grads, feats):
    high, less = (feats[0:HD].astype(jnp.float32), feats[HD:FEAT].astype(jnp.float32))
    grad_high, grad_less = (grads[0:HD], grads[HD:FEAT])
    high_part = high * (grad_high - jnp.sum(high * grad_high, 0, keepdims=True))
    less_part = less * (grad_less - jnp.sum(less * grad_less, 0, keepdims=True))
    return (high_part - less_part).astype(jnp.bfloat16)


def back_call(feat_q, feat_k, value_a, grad_a, memory, later, query_t, key_t, blocks):
    rows = feat_q.shape[2]
    half = rows // 2
    groups = H // 4
    cores = lax.axis_size("tensor")
    split = split_of(3 * D)
    width = 3 * D // split

    def body(fq, fk, va, ga, mem, late, qt, kt, blk, out, own, other, feature, sums, low_q, low_k):
        early = lax.broadcasted_iota(jnp.int32, (half, half), 0)
        after = lax.broadcasted_iota(jnp.int32, (half, half), 1)
        seen = early <= after
        lane = lax.broadcasted_iota(jnp.int32, (HD, FEAT), 1)

        def one_head(head, carry):
            queries, keys, value, grad = (fq[head], fk[head], va[head], ga[head])
            past = mem[head].astype(jnp.bfloat16)
            next_part = late[head].astype(jnp.bfloat16)
            first, cross, last = masked_scores(queries, keys.T)
            value_row = value.T
            top = nn(value_row[0:half], grad)
            corner = nn(value_row[half:], grad[:, half:])
            d_first = jnp.where(seen, top[:, 0:half], 0.0).astype(jnp.bfloat16)
            d_cross = top[:, half:].astype(jnp.bfloat16)
            d_last = jnp.where(seen, corner, 0.0).astype(jnp.bfloat16)
            window = pl.ds(pl.multiple_of(head * HD, HD), HD)
            grad_q = contract_rows(past, grad)
            low_q[window, 0:half] = soft_back(
                grad_q[:, 0:half] + nn(keys[:, 0:half], d_first), queries[:, 0:half]
            )
            low_q[window, half:rows] = soft_back(
                grad_q[:, half:] + nn(keys[:, 0:half], d_cross) + nn(keys[:, half:], d_last),
                queries[:, half:],
            )
            grad_k = contract_rows(next_part, value)
            low_k[window, 0:half] = soft_back(
                grad_k[:, 0:half]
                + contract_cols(queries[:, 0:half], d_first)
                + contract_cols(queries[:, half:], d_cross),
                keys[:, 0:half],
            )
            low_k[window, half:rows] = soft_back(
                grad_k[:, half:] + contract_cols(queries[:, half:], d_last), keys[:, half:]
            )
            grad_v = nn(next_part[0:HD], keys)
            window_v = pl.ds(pl.multiple_of(2 * D + head * HD, HD), HD)
            out[window_v, 0:half] = (
                grad_v[:, 0:half]
                + contract_cols(grad[0:HD, 0:half], first)
                + contract_cols(grad[0:HD, half:], cross)
            ).astype(jnp.bfloat16)
            out[window_v, half:rows] = (
                grad_v[:, half:] + contract_cols(grad[0:HD, half:], last)
            ).astype(jnp.bfloat16)
            return carry

        lax.fori_loop(0, H, one_head, 0)
        for which, low, source in ((0, low_q, qt), (1, low_k, kt)):
            for group in range(groups):
                window = slice(group * 256, (group + 1) * 256)
                out[which * D + group * 256 : which * D + (group + 1) * 256, :] = nn(
                    blk[which * groups + group], low[window, :]
                ).astype(jnp.bfloat16)
            for pair in range(H // 2):
                window = slice(pair * FEAT, (pair + 1) * FEAT)
                both = contract_cols(source[window, :], low[window, :])
                feature[which * (H // 2) + pair] = jnp.where(lane < HD, both[0:HD], both[HD:FEAT])
        ones = jnp.ones((8, rows), jnp.bfloat16)
        sums[...] = contract_cols(ones, out[...])
        core = lax.axis_index("tensor")
        if split > 1:
            own[...] = out[pl.ds(pl.multiple_of(core * width, 128), width), :]
            for step in range(1, split):
                start = lax.rem(core + step, cores) * width
                other[step - 1] = out[pl.ds(pl.multiple_of(start, 128), width), :]
        else:
            own[...] = out[...]
            other[...] = jnp.zeros_like(other)

    low = lambda *shape: jax.ShapeDtypeStruct(shape, jnp.bfloat16)
    return pl.pallas_call(
        body,
        out_shape=(
            low(3 * D, rows),
            low(width, rows),
            low(split - 1, width, rows) if split > 1 else low(1, 16, 128),
            jax.ShapeDtypeStruct((H, HD, FEAT), jnp.float32),
            jax.ShapeDtypeStruct((8, 3 * D), jnp.float32),
        ),
        in_specs=whole(9),
        out_specs=tuple(whole(5)),
        scratch_shapes=[pltpu.VMEM((D, rows), jnp.bfloat16)] * 2,
        compiler_params=pltpu.CompilerParams(vmem_limit_bytes=room),
        cost_estimate=estimate(H * rows * rows * 1500, 15e6),
        name="back",
    )(feat_q, feat_k, value_a, grad_a, memory, later, query_t, key_t, blocks)


def tokens_call(projected_t, grad_resid, tokens, gains, pieces):
    rows = tokens.shape[0]

    def body(*refs):
        proj, res, tok, gain = refs[:4]
        sources = refs[4 : 4 + len(pieces)]
        out, sums = refs[4 + len(pieces) : -3]
        weight, sems, grad_normed = refs[-3:]
        copies = place_copies(sources, weight, sems)
        start_all(copies)
        sums[...] = jnp.zeros_like(sums)
        wait_all(copies)
        grad_normed[...] = nn(flat_rows(weight, 0, 3 * D), proj[...]).T

        def norm_rows(step, carry):
            window = pl.ds(pl.multiple_of(step * 128, 128), 128)
            incoming = grad_normed[window, :]
            normal, scale = normal_parts(tok[window, :].astype(jnp.float32))
            out[window, :] = res[window, :] + norm_back(normal, scale, incoming, gain[0:1, :])
            sums[0:1, :] += jnp.sum(incoming * normal, 0, keepdims=True)
            sums[1:2, :] += jnp.sum(incoming, 0, keepdims=True)
            return carry

        lax.fori_loop(0, rows // 128, norm_rows, 0)

    return pl.pallas_call(
        body,
        out_shape=(
            jax.ShapeDtypeStruct((rows, D), jnp.float32),
            jax.ShapeDtypeStruct((8, D), jnp.float32),
        ),
        in_specs=whole(4) + [far_spec()] * len(pieces),
        out_specs=tuple(whole(2)),
        scratch_shapes=[*placed(pieces), pltpu.VMEM((rows, D), jnp.float32)],
        compiler_params=pltpu.CompilerParams(vmem_limit_bytes=room),
        cost_estimate=estimate(6 * rows * D * D, 10e6),
        name="tokens_back",
    )(projected_t, grad_resid, tokens, gains, *pieces)


MISC = 80


def pack_call(feature, token_sums, mid_sums, late_sums, up_rows):
    half = H * HD // 2

    def body(feat, tok, mid, late, up, mine, other):
        rows = lax.broadcasted_iota(jnp.int32, (8, FEAT), 0)

        def tile_rows(values, column):
            total = jnp.zeros((8, FEAT), jnp.float32)
            for spot, (ref, row, shift) in enumerate(values):
                part = ref[row : row + 1, shift + column * FEAT : shift + (column + 1) * FEAT]
                total = jnp.where(rows == spot, part, total)
            return total

        upper = lax.rem(lax.axis_index("tensor"), 2)
        parts = [(tok, 0, 0), (tok, 1, 0), (mid, 0, 0), (mid, 1, 0), (mid, 2, 0), (mid, 3, 0)]
        parts += [(late, 0, 0), (late, 0, D)]
        first_rows = [tile_rows(parts, column) for column in range(D // FEAT)]
        first_rows.append(jnp.zeros((MISC - 8 * len(first_rows), FEAT), jnp.float32))
        last_rows = [up[...], jnp.zeros((8, FEAT), jnp.float32)]
        last_rows += [tile_rows([(late, 0, 2 * D)], column) for column in range(D // FEAT)]
        first_misc = jnp.concatenate(first_rows, 0).astype(jnp.bfloat16)
        last_misc = jnp.concatenate(last_rows, 0).astype(jnp.bfloat16)
        for target, wanted in ((mine, 0), (other, 1)):

            @pl.when(upper == wanted)
            def lower_half():
                target[0:half, :] = feat[0 : H // 2].reshape(half, FEAT).astype(jnp.bfloat16)
                target[half:, :] = first_misc

            @pl.when(upper != wanted)
            def upper_half():
                target[0:half, :] = feat[H // 2 :].reshape(half, FEAT).astype(jnp.bfloat16)
                target[half:, :] = last_misc

    out = jax.ShapeDtypeStruct((half + MISC, FEAT), jnp.bfloat16)
    return pl.pallas_call(
        body,
        out_shape=(out, out),
        in_specs=whole(5),
        out_specs=tuple(whole(2)),
        compiler_params=pltpu.CompilerParams(vmem_limit_bytes=8 * 1024 * 1024),
        cost_estimate=estimate(0, 1e6),
        name="pack",
    )(feature, token_sums, mid_sums, late_sums, up_rows)


def small_call(mine, other, features, gains, biases, ups):
    half = H * HD // 2

    def body(mine_ref, other_ref, *refs):
        params, outs = (refs[:12], refs[12:])
        upper = lax.rem(lax.axis_index("tensor"), 2) == 1
        own, far = (mine_ref[...].astype(jnp.float32), other_ref[...].astype(jnp.float32))
        low_half = jnp.where(upper, far, own)
        high_half = jnp.where(upper, own, far)

        def update(number, spot, gradient, rate, decay):
            refs_in = params[3 * number : 3 * number + 3]
            new = adam_step(*(ref[spot] for ref in refs_in), gradient, rate, decay)
            for target, value in zip(outs[3 * number : 3 * number + 3], new):
                target[spot] = value

        for which, part in ((0, low_half), (1, high_half)):
            for pair in range(H // 2):
                both = part[pair * HD : (pair + 1) * HD, :]
                update(0, (which, 2 * pair), both[:, 0:HD], rate_feature, decay_rate)
                update(0, (which, 2 * pair + 1), both[:, HD:FEAT], rate_feature, decay_rate)
        for column in range(D // FEAT):
            lanes = slice(column * FEAT, (column + 1) * FEAT)
            tile = low_half[half + 8 * column : half + 8 * column + 8, :]
            begin = half + 32 + 8 * column
            values = high_half[begin : begin + 1, :]
            for row, spot in ((0, 0), (1, 2)):
                window = (slice(row, row + 1), lanes)
                update(1, window, tile[spot : spot + 1, :], rate_vector, 0.0)
            rows = [tile[1:2], tile[3:4], tile[6:7], tile[7:8], values, tile[4:5], tile[5:6]]
            for row, value in enumerate(rows):
                update(2, (slice(row, row + 1), lanes), value, rate_vector, 0.0)
        update(3, (slice(None), slice(None)), high_half[half : half + 24, :], rate_upbias, 0.0)

    flat = [*features, *gains, *biases, *ups]
    return pl.pallas_call(
        body,
        out_shape=tuple(jax.ShapeDtypeStruct(part.shape, jnp.float32) for part in flat),
        in_specs=whole(2 + len(flat)),
        out_specs=tuple(whole(len(flat))),
        compiler_params=pltpu.CompilerParams(vmem_limit_bytes=20 * 1024 * 1024),
        cost_estimate=estimate(0, 6e6),
        name="small",
    )(mine, other, *flat)


def shared_operands(left_t, right_part):
    split = split_of(right_part.shape[1])
    cores = lax.axis_size("tensor")
    if split == 1:
        return ([left_t], [right_part])
    width = right_part.shape[1] // split
    core = lax.axis_index("tensor")
    lefts = [left_t] + [from_core(left_t, step) for step in range(1, split)]
    rights = [lax.dynamic_slice_in_dim(right_part, core * width, width, 1)]
    sent = []
    for step in range(1, split):
        piece = lax.dynamic_slice_in_dim(right_part, (core + step) % cores * width, width, 1)
        sent.append(from_core(piece, cores - step))
    return (lefts, rights + sent[::-1])


def spread_columns(total, columns):
    split = columns // total.shape[1]
    if split == 1:
        return total
    core = lax.axis_index("tensor")
    pieces = [total] + [from_core(total, step) for step in range(1, split)]
    ordered = []
    for target in range(split):
        pick = pieces[0]
        for step in range(1, split):
            pick = jnp.where((core + step) % split == target, pieces[step], pick)
        ordered.append(pick)
    return jnp.concatenate(ordered, 1)


def tie(values, *marks):
    return lax.optimization_barrier((values, marks))[0]


def own_columns(weight):
    split = split_of(weight.shape[1])
    if split > 1:
        width = weight.shape[1] // split
        weight = lax.dynamic_slice_in_dim(weight, lax.axis_index("tensor") * width, width, 1)
    return weight.astype(jnp.bfloat16)


def far_parts(own):
    return [own] + [send_far(own, step) for step in range(1, lax.axis_size("dp") // 4)]


def both_cores(pieces, columns):
    split = columns // pieces[0].shape[2]
    pieces = list(pieces)
    own = pieces
    for offset in range(1, split):
        pieces = pieces + [from_core(piece, offset) for piece in own]
    return pieces


def shards(
    tokens,
    out_grad,
    inward_weight,
    inward_first,
    inward_second,
    outward_weight,
    outward_first,
    outward_second,
    feature_weight,
    feature_first,
    feature_second,
    hidden_weight,
    hidden_first,
    hidden_second,
    norm_gains,
    gains_first,
    gains_second,
    bias_rows,
    biases_first,
    biases_second,
    hidden_bias,
    upbias_first,
    upbias_second,
):
    cores = lax.axis_size("tensor")
    core = lax.axis_index("tensor")
    columns = hidden_weight.shape[2]
    inward_far = far_parts(own_columns(inward_weight))
    outward_own = own_columns(outward_weight)
    plane = [
        outward_own,
        send_first(outward_own),
        send_second(outward_own),
        send(outward_own, lambda place, core: place ^ 3),
    ]
    grads = [out_grad] + [from_core(out_grad, step) for step in range(1, cores)]
    up_far = far_parts(tie(hidden_weight[0].astype(jnp.bfloat16), inward_far))
    (inward_near,) = stack_call(inward_far, [inward_far[0].shape[1]])
    inward_side, inward_next = (send_first(inward_near), send_second(inward_near))
    inward_rest = send_second(inward_side)
    inward = both_cores([inward_near, inward_side, inward_next, inward_rest], 3 * D)
    (outward_plane,) = stack_call(plane, [outward_own.shape[1]])
    outward_parts = far_parts(tie(outward_plane, up_far))
    (up_near,) = stack_call(tie(up_far, inward_rest), [columns])
    up_side, up_next = (send_first(up_near), send_second(up_near))
    norm_t, query_t, key_t, value_a, feat_q, feat_k, update, blocks = features_call(
        tokens, norm_gains, bias_rows, feature_weight.reshape(H // 2, 4 * HD, HD), inward
    )
    memory = carried(update, False)
    down_far = far_parts(tie(hidden_weight[1].astype(jnp.bfloat16), update))
    outward = both_cores(tie(outward_parts, update), D)
    mixed_t, inverse, resid, normed_two = attend_call(
        feat_q, feat_k, value_a, memory, tokens, norm_gains, bias_rows, outward
    )
    up_use = lax.dynamic_slice_in_dim(hidden_bias, core * columns, columns, 0).reshape(1, columns)
    up_side, up_next, down_far = tie((up_side, up_next, down_far), normed_two)
    up = [up_near, up_side, up_next, send_second(up_side)]
    normed = [normed_two] + [from_core(normed_two, step) for step in range(1, cores)]
    (down_near,) = stack_call(down_far, [columns])
    down_side, down_next = (send_first(down_near), send_second(down_near))
    acts = hidden_call(normed, up_use, up)
    down_side, down_next = tie((down_side, down_next), acts[0][0])
    down = [down_near, down_side, down_next, send_second(down_side)]
    pair = product_call(grads, [act[0] for act in acts], False)
    down_rest = scatter_one(*pair)
    runs, up_part = hidden_back_call(acts, grads, up, tie(down, pair[0]))
    mlp_out, back_got = (runs[0][0], 0.0)
    for step in range(1, cores):
        got = from_core(runs[step][1], cores - step)
        back_got = got if step == 1 else back_got + got
        mlp_out = mlp_out + from_core(runs[step][0], cores - step).astype(jnp.float32)
    block_out = (resid + mlp_out + bias_rows[6]).astype(jnp.bfloat16)
    pair = product_call(normed, [run[2] for run in runs], False)
    up_rest = scatter_one(*pair)
    down_rest = scatter_two(tie(down_rest, pair[0]))
    grad_resid, branch, grad_a, part, mid_sums = branch_call(
        runs[0][1],
        tie(back_got, pair[0]),
        out_grad,
        resid,
        mixed_t,
        inverse,
        feat_q,
        norm_gains,
        outward,
    )
    later = carried(part, True)
    down_rest = scatter_three(tie(down_rest, part))
    outward_pairs = shared_operands(mixed_t, branch)
    norm_others = [norm_t] + [from_core(norm_t, step) for step in range(1, cores)]
    projected_t, own_t, other_t, grad_feature, late_sums = back_call(
        feat_q, feat_k, value_a, grad_a, memory, later, query_t, key_t, blocks
    )
    if split_of(3 * D) > 1:
        sent = [from_core(other_t[step - 1], cores - step) for step in range(1, cores)]
        lefts, rights = (norm_others, [own_t] + sent[::-1])
    else:
        lefts, rights = ([norm_t], [projected_t])
    up_rest = scatter_two(tie(up_rest, own_t))
    pair = product_call(*tie(outward_pairs, own_t), None)
    outward_rest = scatter_one(*pair)
    pair = product_call(*tie((lefts, rights), pair[0]), True)
    inward_rest = scatter_one(*pair)
    token_grad, token_sums = tokens_call(
        tie(projected_t, pair[0]), grad_resid, tokens, norm_gains, inward
    )
    up_rows = lax.dynamic_update_slice_in_dim(
        jnp.zeros((FF,), jnp.float32), up_part.reshape(columns), core * columns, 0
    ).reshape(FF // FEAT, FEAT)
    packed = pack_call(grad_feature, token_sums, mid_sums, late_sums, up_rows)
    packed = all_sum(*packed)
    inward_rest = scatter_two(tie(inward_rest, token_sums))
    outward_rest = scatter_two(tie(outward_rest, token_sums))
    up_rest = scatter_three(tie(up_rest, token_sums))
    inward_rest = scatter_three(inward_rest)
    outward_rest = scatter_three(outward_rest)
    grad_down = scatter_sum(tie(down_rest, token_sums))
    grad_up = scatter_sum(up_rest)
    grad_outward = spread_columns(scatter_sum(outward_rest), D)
    grad_inward = spread_columns(scatter_sum(inward_rest), 3 * D)
    small = small_call(
        *packed,
        (feature_weight, feature_first, feature_second),
        (norm_gains, gains_first, gains_second),
        (bias_rows, biases_first, biases_second),
        [part.reshape(FF // FEAT, FEAT) for part in (hidden_bias, upbias_first, upbias_second)],
    )
    feat_w, feat_m, feat_v, gain_w, gain_m, gain_v, bias_w, bias_m, bias_v = small[:9]
    up_w, up_m, up_v = (part.reshape(FF) for part in small[9:])
    grad_hidden = jnp.stack([grad_up, grad_down])
    in_w, in_m, in_v = adam_step(
        inward_weight, inward_first, inward_second, grad_inward, rate_matrix, decay_rate
    )
    out_w, out_m, out_v = adam_step(
        outward_weight, outward_first, outward_second, grad_outward, rate_output, decay_rate
    )
    hid_w, hid_m, hid_v = adam_step(
        hidden_weight, hidden_first, hidden_second, grad_hidden, rate_matrix, decay_rate
    )
    return (
        block_out,
        token_grad,
        in_w,
        in_m,
        in_v,
        out_w,
        out_m,
        out_v,
        feat_w,
        feat_m,
        feat_v,
        hid_w,
        hid_m,
        hid_v,
        gain_w,
        gain_m,
        gain_v,
        bias_w,
        bias_m,
        bias_v,
        up_w,
        up_m,
        up_v,
    )


def solution(mesh):
    placed = (
        P(("dp", "tensor"), None),
        P(("dp", "tensor"), None),
        P("dp", None),
        P("dp", None),
        P("dp", None),
        P("dp", None),
        P("dp", None),
        P("dp", None),
        P(),
        P(),
        P(),
        P(None, "dp", "tensor"),
        P(None, "dp", "tensor"),
        P(None, "dp", "tensor"),
        P(),
        P(),
        P(),
        P(),
        P(),
        P(),
        P(),
        P(),
        P(),
    )

    return jax.shard_map(
        shards,
        mesh=mesh,
        in_specs=placed,
        out_specs=(
            P(("dp", "tensor"), None),
            P(("dp", "tensor"), None),
            P("dp", None),
            P("dp", None),
            P("dp", None),
            P("dp", None),
            P("dp", None),
            P("dp", None),
            P(),
            P(),
            P(),
            P(None, "dp", "tensor"),
            P(None, "dp", "tensor"),
            P(None, "dp", "tensor"),
            P(),
            P(),
            P(),
            P(),
            P(),
            P(),
            P(),
            P(),
            P(),
        ),
        check_vma=False,
    )
```
